32 devices in a mesh: ctx: 8 (over y, x, core), mp: 4 (over z).
Axes of the slice: x: 2, y: 2, z: 4, core: 2. Of those that a mesh axis runs over, the one named last changes fastest.
Arguments:
- tokens: bfloat16 [2048, 4096], P(('ctx', 'mp')), may hold values from -6 to 6
- branch: bfloat16 [2048, 4096], P('ctx', 'mp'), may hold values from -4 to 4
- out_grad: bfloat16 [2048, 4096], P(('ctx', 'mp')), may hold values from -6 to 6
- w_in: bfloat16 [4096, 4096], P(None, 'mp'), may hold values from -0.09375 to 0.09375
- conv_w: bfloat16 [4, 4096], P(None, 'mp'), may hold values from -3 to 3
- gate_a_w: bfloat16 [16, 256, 256], P('mp'), may hold values from -0.375 to 0.375
- gate_a_b: float32 [4096], P('mp'), may hold values from -4 to 4
- gate_i_w: bfloat16 [16, 256, 256], P('mp'), may hold values from -0.375 to 0.375
- gate_i_b: float32 [4096], P('mp'), may hold values from -4 to 4
- decay_param: float32 [4096], P('mp')
- w_out: bfloat16 [4096, 4096], P('mp'), may hold values from -0.09375 to 0.09375
- state_init: float32 [4096], P('mp'), may hold values from -5 to 5
- conv_history: bfloat16 [3, 4096], P(None, 'mp'), may hold values from -5 to 5
Outputs:
- tokens_grad: bfloat16 [2048, 4096], P(('ctx', 'mp'))
- branch_grad: bfloat16 [2048, 4096], P('ctx', 'mp')
- w_in_grad: float32 [4096, 4096], P('ctx', 'mp')
- w_out_grad: float32 [4096, 4096], P('mp', 'ctx')
- conv_w_grad: float32 [4, 4096], P(None, 'mp')
- gate_a_w_grad: float32 [16, 256, 256], P('mp')
- gate_a_b_grad: float32 [4096], P('mp')
- gate_i_w_grad: float32 [16, 256, 256], P('mp')
- gate_i_b_grad: float32 [4096], P('mp')
- decay_grad: float32 [4096], P('mp')
The draws below stay inside these ranges and needn't reach their ends.
All inputs are finite; a program needn't handle non-finite values.
Results may differ from the reference program's by a relative error of at most 0.02.
Values may be sent and summed in bfloat16 or wider, within the bound.
No kernel may reach another device: no remote copies, remote signals or barrier semaphores. Data moves between devices by JAX's collectives and lax.ppermute only.
A program may use at most 128 MiB of HBM per device.

```python
import jax
import jax.numpy as jnp
from jax import lax

D = 4096
DR = 4096
H = 16
CONV = 4
TOK_DEV = 256
TOKENS = 2048
BLOCK = 256
N_CTX = 8
N_MP = 4


def draw_decay_param(key, part):
    key_kind, key_slow, key_fast = jax.random.split(key, 3)
    slow_share = 0.5
    slow = jax.random.uniform(key_kind, (DR,), jnp.float32) < slow_share
    fraction = jnp.exp(jax.random.uniform(key_slow, (DR,), jnp.float32, jnp.log(0.1), 0.0))
    slow_rate = fraction * (2.302585 / (8.0 * TOKENS))
    fast_rate = jnp.exp(jax.random.uniform(key_fast, (DR,), jnp.float32, jnp.log(0.005), jnp.log(0.1)))
    rate = jnp.where(slow, slow_rate, fast_rate)
    return (-jnp.log(jnp.expm1(rate))).astype(jnp.float32)


def with_spikes(values, key, source, target, shards_of, factor):
    owner, partner = [(jnp.arange(values.shape[dim]) // (values.shape[dim] // shards_of)).reshape([-1 if axis == dim else 1 for axis in range(values.ndim)]) for dim in (source, target)]
    chosen = jax.random.permutation(key, shards_of)[partner]
    strong = (owner == chosen) | (owner == (partner + shards_of // 2) % shards_of)
    return jnp.where(strong, factor * values, values)


def block_levels(rng, dims, cuts, smallest, top_value):
    level = 1.0
    for axis_at, parts in cuts:
        steps = jax.random.uniform(jax.random.fold_in(jax.random.fold_in(rng, 6), axis_at), (parts,), jnp.float32, smallest / len(cuts), top_value / len(cuts))
        level = level * jnp.repeat(jnp.exp(steps), dims[axis_at] // parts).reshape((-1,) + (1,) * (len(dims) - 1 - axis_at))
    return level


def bell_draw(own_key, shape, spread, most, shards=(), dtype=jnp.bfloat16):
    result = jax.random.normal(own_key, shape, jnp.float32) * spread
    if len(shards) > 0:
        result = block_levels(own_key, shape, shards, -0.22, 0.18) * result
    return jnp.clip(result, min=-most, max=most).astype(dtype)


def bell_draw_with(stream_key, extent, deviation, limit, cuts, heavy, dtype=jnp.bfloat16):
    array = deviation * jax.random.normal(stream_key, extent, jnp.float32)
    if cuts:
        array = array * block_levels(stream_key, extent, cuts, -0.22, 0.18)
    return jnp.clip(with_spikes(array, jax.random.fold_in(stream_key, 3), *heavy), -limit, limit).astype(dtype)


def setup_inputs(seed: int = 0) -> dict:
    key_list = jax.random.split(jax.random.key(seed), 14)
    tokens = bell_draw(key_list[0], (TOKENS, D), 1.0, 6.0, ((0, 32),))
    branch = bell_draw(key_list[1], (TOKENS, DR), 0.7, 4.0, ((0, 8), (1, 4)))
    out_grad = bell_draw_with(key_list[2], (TOKENS, D), 1.0, 6.0, ((0, 32),), (0, 1, 32, 2.75))
    w_in = bell_draw(key_list[3], (D, DR), D ** -0.5, 0.09375, ((1, 4),))
    conv_w = bell_draw(key_list[4], (CONV, DR), CONV ** -0.5, 3.0, ((1, 4),))
    gate_a_w = bell_draw(key_list[5], (H, BLOCK, BLOCK), BLOCK ** -0.5, 0.375, ((0, 4),))
    gate_a_b = bell_draw(key_list[6], (DR,), 1.0, 4.0, ((0, 4),), jnp.float32)
    gate_i_w = bell_draw(key_list[7], (H, BLOCK, BLOCK), BLOCK ** -0.5, 0.375, ((0, 4),))
    gate_i_b = bell_draw(key_list[8], (DR,), 1.0, 4.0, ((0, 4),), jnp.float32)
    decay_param = draw_decay_param(jax.random.fold_in(key_list[13], 71), 0)
    w_out = bell_draw(key_list[10], (DR, D), DR ** -0.5, 0.09375, ((0, 4),))
    state_init = bell_draw(key_list[11], (DR,), 1.0, 5.0, ((0, 4),), jnp.float32)
    conv_history = bell_draw(key_list[12], (CONV - 1, DR), 1.0, 5.0, ((1, 4),))
    return {"tokens": tokens, "branch": branch, "out_grad": out_grad, "w_in": w_in, "conv_w": conv_w, "gate_a_w": gate_a_w, "gate_a_b": gate_a_b, "gate_i_w": gate_i_w, "gate_i_b": gate_i_b, "decay_param": decay_param, "w_out": w_out, "state_init": state_init, "conv_history": conv_history}


def linear_step(state, pair):
    state = pair[0] * state + pair[1]
    return (state, state)

def adjoint_step(carry, pair):
    adjoint = pair[1] + carry
    return (pair[0] * adjoint, adjoint)

def rounded(value):
    return lax.optimization_barrier(value.astype(jnp.bfloat16)).astype(jnp.float32)

def run_sum(left, right):

    def add_run(total, pair):
        term = jnp.dot(pair[0].T, pair[1], preferred_element_type=jnp.float32)
        return (total + rounded(term), None)
    start = jnp.zeros((left.shape[2], right.shape[2]), jnp.float32)
    total, unused = lax.scan(add_run, start, (left, right))
    return total

def group_backward(tokens, branch, out_grad, w_in, conv_w, gate_a_w, gate_a_b, gate_i_w, gate_i_b, decay_param, w_out, state_init, conv_history):
    length = tokens.shape[0]
    channels = w_in.shape[1]
    blocks = gate_a_w.shape[0]
    block = gate_a_w.shape[1]
    taps = conv_w.shape[0]
    projected = jnp.dot(tokens, w_in, preferred_element_type=jnp.float32).astype(jnp.bfloat16)
    extended = jnp.concatenate([conv_history, projected], 0).astype(jnp.float32)
    kernel = conv_w.astype(jnp.float32)
    conv_sum = jnp.zeros((length, channels), jnp.float32)
    for shift_by in range(taps):
        conv_sum = conv_sum + kernel[shift_by] * extended[taps - 1 - shift_by:taps - 1 - shift_by + length]
    conv_out = conv_sum.astype(jnp.bfloat16)
    conv_wide = conv_out.astype(jnp.float32)
    conv_blocks = conv_wide.reshape(length, blocks, block)
    gate_a = gate_a_w.astype(jnp.float32)
    gate_i = gate_i_w.astype(jnp.float32)
    recur_gate = jax.nn.sigmoid(jnp.einsum('thb,hbc->thc', conv_blocks, gate_a).reshape(length, channels) + gate_a_b)
    input_gate = jax.nn.sigmoid(jnp.einsum('thb,hbc->thc', conv_blocks, gate_i).reshape(length, channels) + gate_i_b)
    softrate = jax.nn.softplus(-decay_param)
    log_decay = -8.0 * recur_gate * softrate
    decay = jnp.exp(log_decay)
    remain = -jnp.expm1(2.0 * log_decay)
    scaler = jnp.sqrt(remain)
    driven = scaler * input_gate * conv_wide
    final_state, states = lax.scan(linear_step, state_init, (decay, driven))
    branch_wide = branch.astype(jnp.float32)
    gated_out = (states * branch_wide).astype(jnp.bfloat16)
    grad_gated = jnp.dot(out_grad, w_out.T, preferred_element_type=jnp.float32)
    branch_grad = (grad_gated * states).astype(jnp.bfloat16)
    state_grad = grad_gated * branch_wide
    last_carry, adjoint = lax.scan(adjoint_step, jnp.zeros((channels,), jnp.float32), (decay, state_grad), reverse=True)
    previous = jnp.concatenate([state_init[None], states[:-1]], 0)
    scaler_grad = adjoint * input_gate * conv_wide
    log_grad = adjoint * previous * decay - 2.0 * decay * decay * scaler_grad / jnp.sqrt(jnp.maximum(4.0 * remain, 1e-06))
    recur_pre = (log_grad * (-8.0 * softrate) * recur_gate * (1.0 - recur_gate)).astype(jnp.bfloat16)
    input_pre = (adjoint * scaler * conv_wide * input_gate * (1.0 - input_gate)).astype(jnp.bfloat16)
    recur_blocks = recur_pre.astype(jnp.float32).reshape(length, blocks, block)
    input_blocks = input_pre.astype(jnp.float32).reshape(length, blocks, block)
    gate_a_w_grad = jnp.einsum('thb,thc->hbc', conv_blocks, recur_blocks)
    gate_i_w_grad = jnp.einsum('thb,thc->hbc', conv_blocks, input_blocks)
    gate_a_b_grad = lax.optimization_barrier(jnp.sum(recur_pre.astype(jnp.float32), 0))
    gate_i_b_grad = lax.optimization_barrier(jnp.sum(input_pre.astype(jnp.float32), 0))
    decay_grad = lax.optimization_barrier(jnp.sum(log_grad * (-8.0 * recur_gate), 0)) * -jax.nn.sigmoid(-decay_param)
    conv_grad = adjoint * scaler * input_gate
    conv_grad = conv_grad + jnp.einsum('thc,hbc->thb', recur_blocks, gate_a).reshape(length, channels)
    conv_grad = conv_grad + jnp.einsum('thc,hbc->thb', input_blocks, gate_i).reshape(length, channels)
    padded = jnp.concatenate([conv_grad, jnp.zeros((taps - 1, channels), jnp.float32)], 0)
    proj_sum = jnp.zeros((length, channels), jnp.float32)
    tap_grads = []
    for shift_by in range(taps):
        proj_sum = proj_sum + kernel[shift_by] * padded[shift_by:shift_by + length]
        tap_grads.append(lax.optimization_barrier(jnp.sum(conv_grad * extended[taps - 1 - shift_by:taps - 1 - shift_by + length], 0)))
    proj_grad = proj_sum.astype(jnp.bfloat16)
    conv_w_grad = jnp.stack(tap_grads, 0)
    return (branch_grad, proj_grad, gated_out, conv_w_grad, gate_a_w_grad, gate_a_b_grad, gate_i_w_grad, gate_i_b_grad, decay_grad)

def reference(tokens, branch, out_grad, w_in, conv_w, gate_a_w, gate_a_b, gate_i_w, gate_i_b, decay_param, w_out, state_init, conv_history):
    channels = DR // N_MP
    blocks = H // N_MP
    token_runs = tokens.reshape(N_CTX, TOK_DEV, D)
    grad_runs = out_grad.reshape(N_CTX, TOK_DEV, D)
    tokens_total = jnp.zeros((TOKENS, D), jnp.float32)
    collected = []
    for group in range(N_MP):
        low = group * channels
        high = low + channels
        w_in_group = w_in[:, low:high]
        results = group_backward(tokens, branch[:, low:high], out_grad, w_in_group, conv_w[:, low:high], gate_a_w[group * blocks:(group + 1) * blocks], gate_a_b[low:high], gate_i_w[group * blocks:(group + 1) * blocks], gate_i_b[low:high], decay_param[low:high], w_out[low:high], state_init[low:high], conv_history[:, low:high])
        proj_grad = results[1]
        gated_out = results[2]
        tokens_total = tokens_total + rounded(jnp.dot(proj_grad, w_in_group.T, preferred_element_type=jnp.float32))
        w_in_grad = run_sum(token_runs, proj_grad.reshape(N_CTX, TOK_DEV, channels))
        w_out_grad = run_sum(gated_out.reshape(N_CTX, TOK_DEV, channels), grad_runs)
        collected.append((results[0], w_in_grad, w_out_grad) + results[3:])
    branch_grad = jnp.concatenate([item[0] for item in collected], 1)
    w_in_grad = jnp.concatenate([item[1] for item in collected], 1)
    w_out_grad = jnp.concatenate([item[2] for item in collected], 0)
    conv_w_grad = jnp.concatenate([item[3] for item in collected], 1)
    gate_a_w_grad = jnp.concatenate([item[4] for item in collected], 0)
    gate_a_b_grad = jnp.concatenate([item[5] for item in collected], 0)
    gate_i_w_grad = jnp.concatenate([item[6] for item in collected], 0)
    gate_i_b_grad = jnp.concatenate([item[7] for item in collected], 0)
    decay_grad = jnp.concatenate([item[8] for item in collected], 0)
    tokens_grad = tokens_total.astype(jnp.bfloat16)
    return (tokens_grad, branch_grad, w_in_grad, w_out_grad, conv_w_grad, gate_a_w_grad, gate_a_b_grad, gate_i_w_grad, gate_i_b_grad, decay_grad)
```

```python
import functools

import jax
import jax.numpy as jnp
from jax import lax
from jax.experimental import pallas as pl
from jax.experimental.pallas import tpu as pltpu
from jax.sharding import PartitionSpec as P

F32 = jnp.float32
BF16 = jnp.bfloat16
ANY = pl.BlockSpec(memory_space=pl.ANY)
CHUNKS = 8
LANES = 128
HALO = 16
SUMS = 16


def shift(value, axis, distance):
    size = lax.axis_size(axis)
    return lax.ppermute(value, axis, [(i, (i + distance) % size) for i in range(size)])


def step(value, axis, distance):
    size = lax.axis_size(axis)
    route = [(i, i + distance) for i in range(size) if 0 <= i + distance < size]
    return lax.ppermute(value, axis, route)


def swap(value, axis, mask):
    return lax.ppermute(value, axis, [(i, i ^ mask) for i in range(lax.axis_size(axis))])


def after(value, *others):
    return lax.optimization_barrier((value,) + others)[0]


def far_first(size):
    return sorted(range(1, size), key=lambda d: -min(d, size - d))


def dot_tn(left, right):
    return lax.dot_general(left, right, (((0,), (0,)), ((), ())), preferred_element_type=F32)


def dot_nt(left, right):
    return lax.dot_general(left, right, (((1,), (1,)), ((), ())), preferred_element_type=F32)


def params(limit=56 << 20):
    return pltpu.CompilerParams(vmem_limit_bytes=limit)


def cost(flops, moved):
    return pl.CostEstimate(flops=flops, bytes_accessed=moved, transcendentals=0)


def lay_out(where, parts, cols, buf, in_sem, out_sem):
    count, rows, width = len(parts), parts[0].shape[0], cols[0].shape[1]
    copies = []
    for d, part in enumerate(parts):
        place = lax.rem(where[0] + count - d, count) * rows
        spot = buf.at[pl.ds(pl.multiple_of(place, rows), rows), :]
        copies.append(pltpu.make_async_copy(part, spot, in_sem.at[d]))
    outs = []
    for k, col in enumerate(cols):
        at = jnp.bitwise_xor(where[1], k) * width
        outs.append(
            pltpu.make_async_copy(
                buf.at[:, pl.ds(pl.multiple_of(at, width), width)], col, out_sem.at[k]
            )
        )

    @pl.when(pl.program_id(0) == 0)
    def _():
        for copy in copies:
            copy.start()
        for copy in copies:
            copy.wait()
        for copy in outs:
            copy.start()

    return outs


def finish(outs):
    @pl.when(pl.program_id(0) == pl.num_programs(0) - 1)
    def _():
        for copy in outs:
            copy.wait()


def grad_body(count, chips, where, *refs):
    parts, w_ref = refs[:count], refs[count]
    out_ref, cols = refs[count + 1], refs[count + 2 : count + 2 + chips]
    buf, in_sem, out_sem = refs[count + 2 + chips :]
    outs = lay_out(where, parts, cols, buf, in_sem, out_sem)
    out_ref[...] = dot_nt(buf[...], w_ref[...])
    finish(outs)


def proj_body(count, chips, where, *refs):
    parts, w_ref = refs[:count], refs[count]
    out_ref, tail_ref = refs[count + 1 : count + 3]
    cols = refs[count + 3 : count + 3 + chips]
    buf, in_sem, out_sem = refs[count + 3 + chips :]
    outs = lay_out(where, parts, cols, buf, in_sem, out_sem)
    made = jnp.dot(buf[...], w_ref[...], preferred_element_type=F32).astype(BF16)
    out_ref[...] = made
    tail_ref[...] = made[made.shape[0] - HALO :]
    finish(outs)


def project(where, parts, weight, chips, backward):
    count, (rows, depth) = len(parts), parts[0].shape
    length = rows * count
    channels = weight.shape[0] if backward else weight.shape[1]
    tile = min(256, channels)
    width = depth // chips
    made = pl.BlockSpec((length, tile), lambda n, s: (0, n))
    shapes = [jax.ShapeDtypeStruct((length, channels), F32 if backward else BF16)]
    specs = [made]
    if not backward:
        shapes.append(jax.ShapeDtypeStruct((HALO, channels), BF16))
        specs.append(pl.BlockSpec((HALO, tile), lambda n, s: (0, n)))
    shapes += [jax.ShapeDtypeStruct((length, width), BF16)] * chips
    specs += [ANY] * chips
    if backward:
        weight_spec = pl.BlockSpec((tile, depth), lambda n, s: (n, 0))
    else:
        weight_spec = pl.BlockSpec((depth, tile), lambda n, s: (0, n))
    return pl.pallas_call(
        functools.partial(grad_body if backward else proj_body, count, chips),
        grid_spec=pltpu.PrefetchScalarGridSpec(
            num_scalar_prefetch=1,
            grid=(channels // tile,),
            in_specs=[ANY] * count + [weight_spec],
            out_specs=specs,
            scratch_shapes=[
                pltpu.VMEM((length, depth), BF16),
                pltpu.SemaphoreType.DMA((count,)),
                pltpu.SemaphoreType.DMA((chips,)),
            ],
        ),
        out_shape=shapes,
        compiler_params=params(),
        cost_estimate=cost(2 * length * depth * channels, 2 * depth * (channels + 2 * length)),
        name="grads" if backward else "project",
    )(where, *parts, weight)


def fill_ext(ext, proj_ref, tail_ref, hist_ref, first):
    length = proj_ref.shape[0]
    taps = hist_ref.shape[0] + 1
    earlier = jnp.where(
        first, hist_ref[...].astype(F32), tail_ref[...].astype(F32)[HALO - (taps - 1) :]
    )
    ext[8 - (taps - 1) : 8, :] = earlier
    ext[8 : 8 + length, :] = proj_ref[...].astype(F32)


def local_body(
    where,
    proj_ref,
    tail_ref,
    hist_ref,
    conv_w_ref,
    ga_ref,
    gi_ref,
    ab_ref,
    ib_ref,
    rate_ref,
    grad_ref,
    branch_ref,
    conv_ref,
    recur_ref,
    input_ref,
    sl_ref,
    dc_ref,
    al_ref,
    qq_ref,
    ends_ref,
    sent_ref,
    halo_ref,
    ext,
    dec,
    drv,
    sgr,
    slr,
    dcr,
    alr,
    qqr,
):
    length = proj_ref.shape[0]
    taps = conv_w_ref.shape[0]
    fill_ext(ext, proj_ref, tail_ref, hist_ref, where[2] == 0)
    kernel = conv_w_ref[...].astype(F32)
    conv_sum = kernel[0:1] * ext[8 : 8 + length, :]
    for j in range(1, taps):
        conv_sum = conv_sum + kernel[j : j + 1] * ext[8 - j : 8 - j + length, :]
    conv_out = conv_sum.astype(BF16)
    conv_ref[...] = conv_out
    conv_wide = conv_out.astype(F32)
    recur = jax.nn.sigmoid(jnp.dot(conv_out, ga_ref[0], preferred_element_type=F32) + ab_ref[...])
    inp = jax.nn.sigmoid(jnp.dot(conv_out, gi_ref[0], preferred_element_type=F32) + ib_ref[...])
    recur_ref[...] = recur
    input_ref[...] = inp
    decay, remain = decays(recur, rate_ref[...])
    driven = jnp.sqrt(remain) * inp * conv_wide
    state_grad = grad_ref[...] * branch_ref[...].astype(F32)
    per = length // CHUNKS
    width = decay.shape[1]
    lanes = dec.shape[2]
    ends = []
    for g in range(width // lanes):
        cut = slice(g * lanes, (g + 1) * lanes)
        dec[g] = decay[:, cut]
        drv[g] = driven[:, cut]
        sgr[g] = state_grad[:, cut]
        state = carry = jnp.zeros((CHUNKS, lanes), F32)
        prod = after_prod = jnp.ones((CHUNKS, lanes), F32)
        for i in range(per):
            rows = pl.ds(i, CHUNKS, stride=per)
            a = dec[g, rows, :]
            state = a * state + drv[g, rows, :]
            prod = a * prod
            slr[g, rows, :] = state
            dcr[g, rows, :] = prod
            back = pl.ds(per - 1 - i, CHUNKS, stride=per)
            b = dec[g, back, :]
            adj = sgr[g, back, :] + carry
            alr[g, back, :] = adj
            qqr[g, back, :] = after_prod
            carry = b * adj
            after_prod = b * after_prod
        for out, kept in zip((sl_ref, dc_ref, al_ref, qq_ref), (slr, dcr, alr, qqr)):
            out[:, cut] = kept[g]
        ends.append((state, prod, carry))
    state, prod, carry = (jnp.concatenate(each, 1) for each in zip(*ends))
    ends_ref[0:8, :] = state
    ends_ref[8:16, :] = prod
    ends_ref[16:24, :] = carry
    total = prod[0:1]
    last = state[0:1]
    for j in range(1, CHUNKS):
        last = prod[j : j + 1] * last + state[j : j + 1]
        total = total * prod[j : j + 1]
    first = carry[CHUNKS - 1 : CHUNKS]
    later = prod[CHUNKS - 1 : CHUNKS]
    for j in range(CHUNKS - 2, 0, -1):
        first = prod[j : j + 1] * first + carry[j : j + 1]
        later = prod[j : j + 1] * later
    into = first
    first = prod[0:1] * first + carry[0:1]
    sent_ref[...] = jnp.concatenate([total, last, first, jnp.zeros((5, width), F32)], 0)
    n = taps - 1
    halo_ref[0:n, :] = conv_wide[0:n]
    halo_ref[n : 2 * n, :] = recur[0:n]
    halo_ref[2 * n : 3 * n, :] = inp[0:n]
    qq = qq_ref[0:n, :]
    halo_ref[3 * n : 4 * n, :] = al_ref[0:n, :] + qq * into
    halo_ref[4 * n : 5 * n, :] = qq * later


def decays(recur, rate):
    log_decay = -8.0 * recur * rate
    decay = jnp.exp(log_decay)
    return decay, -jnp.tanh(log_decay) * (decay * decay + 1.0)


def local(where, projected, tail, hist, conv_w, ga, gi, ab, ib, rate, grad, branch):
    length, channels = projected.shape
    blocks, block = ga.shape[0], ga.shape[1]

    def rows(n):
        return pl.BlockSpec((n, block), lambda i, s: (0, i))

    gate = pl.BlockSpec((1, block, block), lambda i, s: (i, 0, 0))
    full = jax.ShapeDtypeStruct((length, channels), F32)
    return pl.pallas_call(
        local_body,
        grid_spec=pltpu.PrefetchScalarGridSpec(
            num_scalar_prefetch=1,
            grid=(blocks,),
            in_specs=[
                rows(length),
                rows(HALO),
                rows(hist.shape[0]),
                rows(conv_w.shape[0]),
                gate,
                gate,
                rows(1),
                rows(1),
                rows(1),
                rows(length),
                rows(length),
            ],
            out_specs=[rows(length)] * 7 + [rows(24), rows(8), rows(HALO)],
            scratch_shapes=[pltpu.VMEM((length + 8, block), F32)]
            + [pltpu.VMEM((block // LANES, length, LANES), F32)] * 7,
        ),
        out_shape=[jax.ShapeDtypeStruct((length, channels), BF16)]
        + [full] * 6
        + [
            jax.ShapeDtypeStruct((24, channels), F32),
            jax.ShapeDtypeStruct((8, channels), F32),
            jax.ShapeDtypeStruct((HALO, channels), F32),
        ],
        compiler_params=params(),
        cost_estimate=cost(4 * length * channels * block, 34 * length * channels),
        name="local",
    )(where, projected, tail, hist, conv_w, ga, gi, ab, ib, rate, grad, branch)


def gate_grads(adjoint, previous, conv_wide, recur, inp, rate):
    decay, remain = decays(recur, rate)
    scaler = jnp.sqrt(remain)
    scaler_grad = adjoint * inp * conv_wide
    log_grad = adjoint * previous * decay - 2.0 * decay * decay * scaler_grad * lax.rsqrt(
        jnp.maximum(4.0 * remain, 1e-06)
    )
    recur_pre = (log_grad * (-8.0 * rate) * recur * (1.0 - recur)).astype(BF16)
    input_pre = (scaler_grad * scaler * (1.0 - inp)).astype(BF16)
    return log_grad, recur_pre, input_pre, adjoint * scaler * inp


def final_body(
    pairs,
    where,
    *refs,
):
    gathered, refs = refs[: pairs + 1], refs[pairs + 1 :]
    (
        halo_ref,
        init_ref,
        ends_ref,
        proj_ref,
        tail_ref,
        hist_ref,
        conv_w_ref,
        ga_ref,
        gi_ref,
        rate_ref,
        grad_ref,
        branch_ref,
        conv_ref,
        recur_ref,
        input_ref,
        sl_ref,
        dc_ref,
        al_ref,
        qq_ref,
        branch_grad_ref,
        gated_ref,
        proj_grad_ref,
        sums_a_ref,
        sums_i_ref,
        ext,
        cgr,
        adj,
        prev,
        got,
    ) = refs
    length, width = proj_ref.shape
    taps = conv_w_ref.shape[0]
    n = taps - 1
    me = where[2]
    count = 2 * pairs
    got[0, :, :] = gathered[0][...]
    got[1, :, :] = gathered[1][...]
    for p in range(1, pairs):
        got[2 * p, :, :] = gathered[p + 1][0:8, :]
        got[2 * p + 1, :, :] = gathered[p + 1][8:16, :]
    state_in = init_ref[...]
    for c in range(count - 1):
        item = got.at[jnp.bitwise_xor(me, c)]
        state_in = jnp.where(c < me, item[0:1, :] * state_in + item[1:2, :], state_in)
    carry_in = jnp.zeros((1, width), F32)
    next_in = jnp.zeros((1, width), F32)
    for c in range(count - 1, 0, -1):
        item = got.at[jnp.bitwise_xor(me, c)]
        longer = item[0:1, :] * carry_in + item[2:3, :]
        next_in = jnp.where(c == me + 1, carry_in, next_in)
        carry_in = jnp.where(c > me, longer, carry_in)
    per = length // CHUNKS
    enter = state_in
    prev[7:8, :] = state_in
    for j in range(CHUNKS):
        rows = slice(j * per, (j + 1) * per)
        prev[8 + j * per : 8 + (j + 1) * per, :] = sl_ref[rows, :] + dc_ref[rows, :] * enter
        enter = ends_ref[8 + j : 9 + j, :] * enter + ends_ref[j : j + 1, :]
    back = carry_in
    for j in range(CHUNKS - 1, -1, -1):
        rows = slice(j * per, (j + 1) * per)
        adj[rows, :] = al_ref[rows, :] + qq_ref[rows, :] * back
        back = ends_ref[8 + j : 9 + j, :] * back + ends_ref[16 + j : 17 + j, :]
    states = prev[8 : 8 + length, :]
    gated_ref[...] = (states * branch_ref[...].astype(F32)).astype(BF16)
    branch_grad_ref[...] = (grad_ref[...] * states).astype(BF16)
    rate = rate_ref[...]
    conv_out = conv_ref[...]
    recur = recur_ref[...]
    log_grad, recur_pre, input_pre, direct = gate_grads(
        adj[...], prev[7 : 7 + length, :], conv_out.astype(F32), recur, input_ref[...], rate
    )
    conv_grad = direct + dot_nt(recur_pre, ga_ref[0]) + dot_nt(input_pre, gi_ref[0])
    cgr[0:length, :] = conv_grad
    conv_n, recur_n, inp_n = (halo_ref[k * n : (k + 1) * n, :] for k in range(3))
    adj_n = halo_ref[3 * n : 4 * n, :] + halo_ref[4 * n : 5 * n, :] * next_in
    decay_n, remain_n = decays(recur_n, rate)
    drive_n = jnp.sqrt(remain_n) * inp_n * conv_n
    run = states[length - 1 : length]
    before = [run]
    for t in range(n - 1):
        run = decay_n[t : t + 1] * run + drive_n[t : t + 1]
        before.append(run)
    _, recur_e, input_e, direct_e = gate_grads(
        adj_n, jnp.concatenate(before, 0), conv_n, recur_n, inp_n, rate
    )
    empty = jnp.zeros((8 - n, width), F32)

    def padded(value):
        return jnp.concatenate([value.astype(F32), empty], 0)

    ext_grad = (
        padded(direct_e)
        + dot_nt(padded(recur_e).astype(BF16), ga_ref[0])
        + dot_nt(padded(input_e).astype(BF16), gi_ref[0])
    )
    cgr[length : length + 8, :] = jnp.where(me == count - 1, 0.0, ext_grad)
    fill_ext(ext, proj_ref, tail_ref, hist_ref, me == 0)
    kernel = conv_w_ref[...].astype(F32)
    proj_sum = kernel[0:1] * conv_grad
    tap_sums = [jnp.sum(conv_grad * ext[8 : 8 + length, :], 0, keepdims=True)]
    for j in range(1, taps):
        proj_sum = proj_sum + kernel[j : j + 1] * cgr[j : j + length, :]
        tap_sums.append(jnp.sum(conv_grad * ext[8 - j : 8 - j + length, :], 0, keepdims=True))
    proj_grad_ref[...] = proj_sum.astype(BF16)
    sums_a_ref[0, 0:width, :] = dot_tn(conv_out, recur_pre).astype(BF16)
    sums_i_ref[0, 0:width, :] = dot_tn(conv_out, input_pre).astype(BF16)
    other_sums = [
        jnp.sum(log_grad * (-8.0 * recur), 0, keepdims=True),
        jnp.sum(recur_pre.astype(F32), 0, keepdims=True),
        jnp.sum(input_pre.astype(F32), 0, keepdims=True),
    ]
    pad_a = jnp.zeros((SUMS - taps, width), F32)
    pad_i = jnp.zeros((SUMS - 3, width), F32)
    sums_a_ref[0, width : width + SUMS, :] = jnp.concatenate(tap_sums + [pad_a], 0).astype(BF16)
    sums_i_ref[0, width : width + SUMS, :] = jnp.concatenate(other_sums + [pad_i], 0).astype(BF16)


def final(where, gathered, halo, init, ends, projected, tail, hist, conv_w, ga, gi, rate, grad, branch, kept):
    length, channels = projected.shape
    blocks, block = ga.shape[0], ga.shape[1]
    pairs = len(gathered) - 1

    def rows(n):
        return pl.BlockSpec((n, block), lambda i, s: (0, i))

    gate = pl.BlockSpec((1, block, block), lambda i, s: (i, 0, 0))
    sums = pl.BlockSpec((1, block + SUMS, block), lambda i, s: (i, 0, 0))
    half = jax.ShapeDtypeStruct((length, channels), BF16)
    summed = jax.ShapeDtypeStruct((blocks, block + SUMS, block), BF16)
    return pl.pallas_call(
        functools.partial(final_body, pairs),
        grid_spec=pltpu.PrefetchScalarGridSpec(
            num_scalar_prefetch=1,
            grid=(blocks,),
            in_specs=[rows(g.shape[0]) for g in gathered]
            + [
                rows(HALO),
                rows(1),
                rows(24),
                rows(length),
                rows(HALO),
                rows(hist.shape[0]),
                rows(conv_w.shape[0]),
                gate,
                gate,
                rows(1),
                rows(length),
                rows(length),
            ]
            + [rows(length)] * 7,
            out_specs=[rows(length)] * 3 + [sums] * 2,
            scratch_shapes=[
                pltpu.VMEM((length + 8, block), F32),
                pltpu.VMEM((length + 8, block), F32),
                pltpu.VMEM((length, block), F32),
                pltpu.VMEM((length + 8, block), F32),
                pltpu.VMEM((2 * pairs, 8, block), F32),
            ],
        ),
        out_shape=[half, half, half, summed, summed],
        compiler_params=params(),
        cost_estimate=cost(8 * length * channels * block, 40 * length * channels),
        name="final",
    )(where, *gathered, halo, init, ends, projected, tail, hist, conv_w, ga, gi, rate, grad, branch, *kept)


def back_body(count, where, pg_ref, w_ref, *refs):
    outs, acc = refs[:count], refs[count]
    rows = outs[0].shape[0]
    acc[...] = dot_nt(pg_ref[...], w_ref[...])
    for d, out in enumerate(outs):
        place = lax.rem(where[0] + d, count) * rows
        out[...] = acc[pl.ds(pl.multiple_of(place, rows), rows), :].astype(BF16)


def token_parts(where, proj_grad, w_in, count):
    length, channels = proj_grad.shape
    depth = w_in.shape[0]
    tile = min(1024, depth)
    rows = length // count
    return pl.pallas_call(
        functools.partial(back_body, count),
        grid_spec=pltpu.PrefetchScalarGridSpec(
            num_scalar_prefetch=1,
            grid=(depth // tile,),
            in_specs=[
                pl.BlockSpec((length, channels), lambda n, s: (0, 0)),
                pl.BlockSpec((tile, channels), lambda n, s: (n, 0)),
            ],
            out_specs=[pl.BlockSpec((rows, tile), lambda n, s: (0, n))] * count,
            scratch_shapes=[pltpu.VMEM((length, tile), F32)],
        ),
        out_shape=[jax.ShapeDtypeStruct((rows, depth), BF16)] * count,
        compiler_params=params(),
        cost_estimate=cost(2 * length * depth * channels, 2 * depth * (channels + length)),
        name="back",
    )(where, proj_grad, w_in)


def spread(parts, axis):
    return [parts[0]] + [swap(part, axis, 2 * k) for k, part in enumerate(parts) if k > 0]


def gather_z(value, axis):
    size = lax.axis_size(axis)
    parts = [value] + [None] * (size - 1)
    for d in far_first(size):
        parts[d] = shift(value, axis, d)
    return parts


def shards(
    tokens,
    branch,
    out_grad,
    w_in,
    conv_w,
    gate_a_w,
    gate_a_b,
    gate_i_w,
    gate_i_b,
    decay_param,
    w_out,
    state_init,
    conv_history,
):
    groups, runs = lax.axis_size("mp"), lax.axis_size("ctx")
    chips = runs // 2
    here, run = lax.axis_index("mp"), lax.axis_index("ctx")
    core = lax.rem(run, 2)
    where = jnp.stack([here, run // 2, run, core]).astype(jnp.int32)
    channels = w_in.shape[1]
    blocks, block = gate_a_w.shape[0], gate_a_w.shape[1]
    taps = conv_w.shape[0]
    rate = jax.nn.softplus(-decay_param).reshape(1, channels)
    slope = -jax.nn.sigmoid(-decay_param)
    a_b, i_b = gate_a_b.reshape(1, channels), gate_i_b.reshape(1, channels)
    init = state_init.reshape(1, channels)

    grad_parts = gather_z(out_grad, "mp")
    tokens_late = after(tokens, *grad_parts[1:])
    grad, *grad_cols = project(where, grad_parts, w_out, chips, True)
    token_parts_in = gather_z(tokens_late, "mp")
    grad_cols = spread(grad_cols, "ctx")
    projected, tail, *token_cols = project(where, token_parts_in, w_in, chips, False)
    tail = step(tail, "ctx", 1)
    *kept, ends, sent, halo = local(
        where, projected, tail, conv_history, conv_w, gate_a_w, gate_i_w, a_b, i_b, rate, grad, branch
    )
    paired = swap(sent, "ctx", 1)
    both = jnp.concatenate([sent, paired], 0)
    gathered = [sent, paired] + [swap(both, "ctx", 2 * k) for k in range(1, chips)]
    halo = step(halo, "ctx", -1)
    branch_grad, gated, proj_grad, sums_a, sums_i = final(
        where, gathered, halo, init, ends, projected, tail, conv_history, conv_w,
        gate_a_w, gate_i_w, rate, grad, branch, kept,
    )
    parts_out = token_parts(where, proj_grad, w_in, groups)
    received = [parts_out[0]] + [
        shift(parts_out[d], "mp", d) for d in far_first(groups)
    ]
    tokens_grad = sum(part.astype(F32) for part in received).astype(BF16)

    proj_all = spread([proj_grad] * chips, "ctx")
    token_cols = spread(token_cols, "ctx")
    gated_all = spread([gated] * chips, "ctx")

    grad_cols, gated_all = jnp.concatenate(grad_cols, 0), jnp.concatenate(gated_all, 0)
    token_cols, proj_all = jnp.concatenate(token_cols, 0), jnp.concatenate(proj_all, 0)
    half = grad_cols.shape[1] // 2

    def mine(value, at):
        return lax.dynamic_slice_in_dim(value, at * half, half, 1)

    other_out = dot_tn(gated_all, mine(grad_cols, 1 - core)).astype(BF16)
    other_in = dot_tn(mine(token_cols, 1 - core), proj_all).astype(BF16)
    w_out_grad = dot_tn(gated_all, mine(grad_cols, core)) + swap(other_out, "ctx", 1).astype(F32)
    w_in_grad = dot_tn(mine(token_cols, core), proj_all) + swap(other_in, "ctx", 1).astype(F32)

    sums_mine = jnp.where(core == 0, sums_a, sums_i).astype(F32)
    sums_other = jnp.where(core == 0, sums_i, sums_a)
    chip_sum = (sums_mine + swap(sums_other, "ctx", 1).astype(F32)).astype(BF16)
    rows = blocks * (block + SUMS) // chips
    pieces = chip_sum.reshape(chips, rows, block)
    chip = run // 2
    total = lax.dynamic_index_in_dim(pieces, chip, 0, False).astype(F32)
    for k in range(1, chips):
        piece = lax.dynamic_index_in_dim(pieces, jnp.bitwise_xor(chip, k), 0, False)
        total = total + swap(piece, "ctx", 2 * k).astype(F32)
    total = total.astype(BF16)
    result = jnp.zeros((chips, rows, block), BF16)
    result = lax.dynamic_update_index_in_dim(result, total, chip, 0)
    for k in range(1, chips):
        result = lax.dynamic_update_index_in_dim(
            result, swap(total, "ctx", 2 * k), jnp.bitwise_xor(chip, k), 0
        )
    result = result.reshape(blocks, block + SUMS, block)
    partner = swap(result, "ctx", 1)
    all_a = jnp.where(core == 0, result, partner).astype(F32)
    all_i = jnp.where(core == 0, partner, result).astype(F32)
    conv_w_grad = all_a[:, block : block + taps].transpose(1, 0, 2).reshape(taps, channels)
    rate_total = all_i[:, block].reshape(channels)
    return (
        tokens_grad,
        branch_grad,
        w_in_grad,
        w_out_grad,
        conv_w_grad,
        all_a[:, :block],
        all_i[:, block + 1].reshape(channels),
        all_i[:, :block],
        all_i[:, block + 2].reshape(channels),
        rate_total * slope,
    )


def solution(mesh):
    placed = (
        P(("ctx", "mp"), None),
        P("ctx", "mp"),
        P(("ctx", "mp"), None),
        P(None, "mp"),
        P(None, "mp"),
        P("mp", None, None),
        P("mp"),
        P("mp", None, None),
        P("mp"),
        P("mp"),
        P("mp", None),
        P("mp"),
        P(None, "mp"),
    )
    return jax.shard_map(
        shards,
        mesh=mesh,
        in_specs=placed,
        out_specs=(
            P(("ctx", "mp"), None),
            P("ctx", "mp"),
            P("ctx", "mp"),
            P("mp", "ctx"),
            P(None, "mp"),
            P("mp", None, None),
            P("mp"),
            P("mp", None, None),
            P("mp"),
            P("mp"),
        ),
        check_vma=False,
    )
```

```python
import functools

import jax
import jax.numpy as jnp
from jax import lax
from jax.experimental import pallas as pl
from jax.experimental.pallas import tpu as pltpu
from jax.sharding import PartitionSpec as P


F32 = jnp.float32
BF16 = jnp.bfloat16
ANY = pl.BlockSpec(memory_space=pl.ANY)
HBM = pl.BlockSpec(memory_space=pltpu.HBM)
CHUNKS = 8
LANES = 128
HALO = 16
SUMS = 16


def shift(value, axis, distance):
    size = lax.axis_size(axis)
    return lax.ppermute(value, axis, [(i, (i + distance) % size) for i in range(size)])


def step(value, axis, distance):
    size = lax.axis_size(axis)
    route = [(i, i + distance) for i in range(size) if 0 <= i + distance < size]
    return lax.ppermute(value, axis, route)


def swap(value, axis, mask):
    return lax.ppermute(value, axis, [(i, i ^ mask) for i in range(lax.axis_size(axis))])


def far_first(size):
    return sorted(range(1, size), key=lambda d: -min(d, size - d))


def dot_tn(left, right):
    return lax.dot_general(left, right, (((0,), (0,)), ((), ())), preferred_element_type=F32)


def dot_nt(left, right):
    return lax.dot_general(left, right, (((1,), (1,)), ((), ())), preferred_element_type=F32)


def params(limit=60 << 20):
    return pltpu.CompilerParams(vmem_limit_bytes=limit)


def cost(flops, moved):
    return pl.CostEstimate(flops=flops, bytes_accessed=moved, transcendentals=0)


def weights(ref, held, sem, axis):
    count, tile = held.shape[0], held.shape[1 + axis]
    copies = []
    for n in range(count):
        cut = pl.ds(n * tile, tile)
        copies.append(
            pltpu.make_async_copy(
                ref.at[cut, :] if axis == 0 else ref.at[:, cut], held.at[n], sem.at[n]
            )
        )
    return copies


def ready(copies):
    for n, copy in enumerate(copies):
        pl.when(pl.program_id(0) == n)(copy.wait)


def placing(here, parts, count, into):
    if len(parts) == count:
        copies = [into(part, -d) for d, part in enumerate(parts)]
        for copy in sum(copies, []):
            copy.start()
        return sum(copies, [])

    def start(part, distance):
        for copy in into(part, distance):
            copy.start()

    own, far, plus, minus, relayed = parts
    start(own, 0)
    start(far, 2)
    pl.when(here >= 1)(lambda: start(plus, -1))
    pl.when(here < 1)(lambda: start(relayed, -1))
    pl.when(here < count - 1)(lambda: start(minus, 1))
    pl.when(here >= count - 1)(lambda: start(relayed, 1))
    return into(own, 0) + into(far, 2) + into(plus, -1) + into(minus, 1)


def lay_out(where, parts, cols, buf, in_sem, out_sem, extra=()):
    rows = parts[0].shape[0]
    count = buf.shape[0] // rows
    here = where[0]

    def into(part, distance):
        place = lax.rem(here + count + distance, count)
        spot = buf.at[pl.ds(pl.multiple_of(place * rows, rows), rows), :]
        return [pltpu.make_async_copy(part, spot, in_sem.at[distance % count])]

    outs = []
    for k, col in enumerate(cols):
        width = col.shape[1]
        at = jnp.bitwise_xor(where[1], k) * width
        outs.append(
            pltpu.make_async_copy(
                buf.at[:, pl.ds(pl.multiple_of(at, width), width)], col, out_sem.at[k]
            )
        )

    @pl.when(pl.program_id(0) == 0)
    def _():
        copies = placing(here, parts, count, into)
        for copy in extra:
            copy.start()
        for copy in copies:
            copy.wait()
        for copy in outs:
            copy.start()

    return outs


def weigh_body(kind, chips, groups, parts, where, *refs):
    lefts, refs = refs[:chips], refs[chips:]
    rights, (other_ref, mine_ref, left, right, l_sem, r_sem) = refs[:parts], refs[parts:]
    run = left.shape[0] // chips
    rows = run // groups
    here, core = where[0], where[3]

    def into(part, distance):
        place = lax.rem(here + groups + distance, groups)
        return [
            pltpu.make_async_copy(
                part.at[pl.ds(k * rows, rows), :],
                right.at[pl.ds(pl.multiple_of(k * run + place * rows, rows), rows), :],
                r_sem.at[distance % groups],
            )
            for k in range(chips)
        ]

    @pl.when(pl.program_id(0) == 0)
    def _():
        copies = [
            pltpu.make_async_copy(piece, left.at[pl.ds(k * run, run), :], l_sem.at[k])
            for k, piece in enumerate(lefts)
        ]
        if kind == "out":
            for copy in copies:
                copy.start()
            copies += placing(here, rights, groups, into)
        else:
            copies += [
                pltpu.make_async_copy(piece, right.at[pl.ds(k * run, run), :], r_sem.at[k])
                for k, piece in enumerate(rights)
            ]
            for copy in copies:
                copy.start()
        for copy in copies:
            copy.wait()

    n = pl.program_id(0)
    if kind == "out":
        tile = other_ref.shape[0]
        half = other_ref.shape[1]
        lhs = left[:, pl.ds(pl.multiple_of(n * tile, tile), tile)]
        other = right[:, pl.ds(pl.multiple_of((1 - core) * half, half), half)]
        mine = right[:, pl.ds(pl.multiple_of(core * half, half), half)]
        other_ref[...] = dot_tn(lhs, other).astype(BF16)
        mine_ref[...] = dot_tn(lhs, mine)
    else:
        tile = other_ref.shape[0]
        half = left.shape[1] // 2
        other = left[:, pl.ds(pl.multiple_of((1 - core) * half + n * tile, tile), tile)]
        mine = left[:, pl.ds(pl.multiple_of(core * half + n * tile, tile), tile)]
        other_ref[...] = dot_tn(other, right[...]).astype(BF16)
        mine_ref[...] = dot_tn(mine, right[...])


def weigh(where, lefts, rights, kind, groups):
    chips = len(lefts)
    run, left = lefts[0].shape
    right = rights[0].shape[1]
    if kind == "out":
        high, wide = left, right // 2
    else:
        high, wide = left // 2, right
    tile = min(256, high)
    spec = pl.BlockSpec((tile, wide), lambda n, s: (n, 0))
    return pl.pallas_call(
        functools.partial(weigh_body, kind, chips, groups, len(rights)),
        grid_spec=pltpu.PrefetchScalarGridSpec(
            num_scalar_prefetch=1,
            grid=(high // tile,),
            in_specs=[ANY] * (chips + len(rights)),
            out_specs=[spec, spec],
            scratch_shapes=[
                pltpu.VMEM((chips * run, left), BF16),
                pltpu.VMEM((chips * run, right), BF16),
                pltpu.SemaphoreType.DMA((chips,)),
                pltpu.SemaphoreType.DMA((max(chips, groups),)),
            ],
        ),
        out_shape=[
            jax.ShapeDtypeStruct((high, wide), BF16),
            jax.ShapeDtypeStruct((high, wide), F32),
        ],
        compiler_params=params(),
        cost_estimate=cost(2 * chips * run * left * right, 2 * chips * run * (left + right)),
    )(where, *lefts, *rights)


def finish(outs):
    @pl.when(pl.program_id(0) == pl.num_programs(0) - 1)
    def _():
        for copy in outs:
            copy.wait()


def grad_body(count, where, *refs):
    parts, refs = refs[:count], refs[count:]
    w_ref, dec_ref, qq_ref, prod_ref, branch_ref, grad_ref, al_ref, ends_ref, sent_ref = refs[:9]
    buf, held, dec, sgr, alr, in_sem, w_sem = refs[9:]
    loads = weights(w_ref, held, w_sem, 0)
    lay_out(where, parts, (), buf, in_sem, None, loads)
    ready(loads)
    grad = dot_nt(buf[...], held[pl.program_id(0)])
    grad_ref[...] = grad
    state_grad = grad * branch_ref[...].astype(F32)
    length, width = grad.shape
    per, lanes = length // CHUNKS, dec.shape[2]
    ends = []
    for g in range(width // lanes):
        cut = slice(g * lanes, (g + 1) * lanes)
        dec[g] = dec_ref[:, cut]
        sgr[g] = state_grad[:, cut]
        carry = jnp.zeros((CHUNKS, lanes), F32)
        for i in range(per):
            back = pl.ds(per - 1 - i, CHUNKS, stride=per)
            adj = sgr[g, back, :] + carry
            alr[g, back, :] = adj
            carry = dec[g, back, :] * adj
        al_ref[:, cut] = alr[g]
        ends.append(carry)
    carry = jnp.concatenate(ends, 1)
    ends_ref[...] = carry
    first = carry[CHUNKS - 1 : CHUNKS]
    for j in range(CHUNKS - 2, 0, -1):
        first = prod_ref[8 + j : 9 + j, :] * first + carry[j : j + 1]
    sent_ref[0:1, :] = prod_ref[8:9, :] * first + carry[0:1]
    sent_ref[1:8, :] = al_ref[0:7, :] + qq_ref[0:7, :] * first


def proj_body(count, chips, where, *refs):
    parts, w_ref = refs[:count], refs[count]
    out_ref, tail_ref = refs[count + 1 : count + 3]
    cols = refs[count + 3 : count + 3 + chips]
    buf, held, in_sem, out_sem, w_sem = refs[count + 3 + chips :]
    loads = weights(w_ref, held, w_sem, 1)
    outs = lay_out(where, parts, cols, buf, in_sem, out_sem, loads)
    ready(loads)
    made = jnp.dot(buf[...], held[pl.program_id(0)], preferred_element_type=F32).astype(BF16)
    out_ref[...] = made
    tail_ref[...] = made[made.shape[0] - HALO :]
    finish(outs)


def project(where, parts, weight, groups, chips):
    rows, depth = parts[0].shape
    length, channels = rows * groups, weight.shape[1]
    tile = min(256, channels)
    return pl.pallas_call(
        functools.partial(proj_body, len(parts), chips),
        grid_spec=pltpu.PrefetchScalarGridSpec(
            num_scalar_prefetch=1,
            grid=(channels // tile,),
            in_specs=[ANY] * len(parts) + [HBM],
            out_specs=[
                pl.BlockSpec((length, tile), lambda n, s: (0, n)),
                pl.BlockSpec((HALO, tile), lambda n, s: (0, n)),
            ]
            + [ANY] * chips,
            scratch_shapes=[
                pltpu.VMEM((length, depth), BF16),
                pltpu.VMEM((channels // tile, depth, tile), BF16),
                pltpu.SemaphoreType.DMA((groups,)),
                pltpu.SemaphoreType.DMA((chips,)),
                pltpu.SemaphoreType.DMA((channels // tile,)),
            ],
        ),
        out_shape=[
            jax.ShapeDtypeStruct((length, channels), BF16),
            jax.ShapeDtypeStruct((HALO, channels), BF16),
        ]
        + [jax.ShapeDtypeStruct((length, depth // chips), BF16)] * chips,
        compiler_params=params(),
        cost_estimate=cost(2 * length * depth * channels, 2 * depth * (channels + 2 * length)),
        name="project",
    )(where, *parts, weight)


def grads(where, parts, weight, dec, qq, prod, branch, groups):
    rows, depth = parts[0].shape
    length, channels = rows * groups, weight.shape[0]
    tile = min(256, channels)

    def tall(n):
        return pl.BlockSpec((n, tile), lambda n, s: (0, n))

    full = jax.ShapeDtypeStruct((length, channels), F32)
    few = jax.ShapeDtypeStruct((CHUNKS, channels), F32)
    return pl.pallas_call(
        functools.partial(grad_body, len(parts)),
        grid_spec=pltpu.PrefetchScalarGridSpec(
            num_scalar_prefetch=1,
            grid=(channels // tile,),
            in_specs=[ANY] * len(parts)
            + [HBM]
            + [tall(length), tall(8), tall(16), tall(length)],
            out_specs=[tall(length), tall(length), tall(CHUNKS), tall(8)],
            scratch_shapes=[
                pltpu.VMEM((length, depth), BF16),
                pltpu.VMEM((channels // tile, tile, depth), BF16),
            ]
            + [pltpu.VMEM((tile // LANES, length, LANES), F32)] * 3
            + [pltpu.SemaphoreType.DMA((n,)) for n in (groups, channels // tile)],
        ),
        out_shape=[full, full, few, few],
        compiler_params=params(),
        cost_estimate=cost(2 * length * depth * channels, 2 * depth * (channels + 2 * length)),
        name="grads",
    )(where, *parts, weight, dec, qq, prod, branch)


def fill_ext(ext, proj_ref, tail_ref, hist_ref, first):
    length = proj_ref.shape[0]
    taps = hist_ref.shape[0] + 1
    earlier = jnp.where(
        first, hist_ref[...].astype(F32), tail_ref[...].astype(F32)[HALO - (taps - 1) :]
    )
    ext[8 - (taps - 1) : 8, :] = earlier
    ext[8 : 8 + length, :] = proj_ref[...].astype(F32)


def local_body(
    where,
    proj_ref,
    tail_ref,
    hist_ref,
    conv_w_ref,
    ga_ref,
    gi_ref,
    ab_ref,
    ib_ref,
    rate_ref,
    conv_ref,
    recur_ref,
    input_ref,
    dec_ref,
    sl_ref,
    dc_ref,
    qq_ref,
    ends_ref,
    sent_ref,
    halo_ref,
    ext,
    dec,
    drv,
    slr,
    dcr,
    qqr,
):
    length = proj_ref.shape[0]
    taps = conv_w_ref.shape[0]
    fill_ext(ext, proj_ref, tail_ref, hist_ref, where[2] == 0)
    kernel = conv_w_ref[...].astype(F32)
    conv_sum = kernel[0:1] * ext[8 : 8 + length, :]
    for j in range(1, taps):
        conv_sum = conv_sum + kernel[j : j + 1] * ext[8 - j : 8 - j + length, :]
    conv_out = conv_sum.astype(BF16)
    conv_ref[...] = conv_out
    conv_wide = conv_out.astype(F32)
    recur = jax.nn.sigmoid(jnp.dot(conv_out, ga_ref[0], preferred_element_type=F32) + ab_ref[...])
    inp = jax.nn.sigmoid(jnp.dot(conv_out, gi_ref[0], preferred_element_type=F32) + ib_ref[...])
    recur_ref[...] = recur
    input_ref[...] = inp
    decay, remain = decays(recur, rate_ref[...])
    dec_ref[...] = decay
    driven = jnp.sqrt(remain) * inp * conv_wide
    per = length // CHUNKS
    width = decay.shape[1]
    lanes = dec.shape[2]
    ends = []
    for g in range(width // lanes):
        cut = slice(g * lanes, (g + 1) * lanes)
        dec[g] = decay[:, cut]
        drv[g] = driven[:, cut]
        state = jnp.zeros((CHUNKS, lanes), F32)
        prod = after_prod = jnp.ones((CHUNKS, lanes), F32)
        for i in range(per):
            rows = pl.ds(i, CHUNKS, stride=per)
            a = dec[g, rows, :]
            state = a * state + drv[g, rows, :]
            prod = a * prod
            slr[g, rows, :] = state
            dcr[g, rows, :] = prod
            back = pl.ds(per - 1 - i, CHUNKS, stride=per)
            qqr[g, back, :] = after_prod
            after_prod = dec[g, back, :] * after_prod
        for out, kept in zip((sl_ref, dc_ref, qq_ref), (slr, dcr, qqr)):
            out[:, cut] = kept[g]
        ends.append((state, prod))
    state, prod = (jnp.concatenate(each, 1) for each in zip(*ends))
    ends_ref[0:8, :] = state
    ends_ref[8:16, :] = prod
    total = later = prod[0:1]
    last = state[0:1]
    for j in range(1, CHUNKS):
        last = prod[j : j + 1] * last + state[j : j + 1]
        total = total * prod[j : j + 1]
        later = prod[j : j + 1] if j == 1 else later * prod[j : j + 1]
    sent_ref[...] = jnp.concatenate([total, last, jnp.zeros((6, width), F32)], 0)
    n = taps - 1
    halo_ref[0:n, :] = conv_wide[0:n]
    halo_ref[n : 2 * n, :] = recur[0:n]
    halo_ref[2 * n : 3 * n, :] = inp[0:n]
    halo_ref[3 * n : 4 * n, :] = qq_ref[0:n, :] * later
    halo_ref[4 * n :, :] = jnp.zeros((HALO - 4 * n, width), F32)


def decays(recur, rate):
    log_decay = -8.0 * recur * rate
    decay = jnp.exp(log_decay)
    return decay, -jnp.tanh(log_decay) * (decay * decay + 1.0)


def local(where, projected, tail, hist, conv_w, ga, gi, ab, ib, rate):
    length, channels = projected.shape
    blocks, block = ga.shape[0], ga.shape[1]

    def rows(n):
        return pl.BlockSpec((n, block), lambda i, s: (0, i))

    gate = pl.BlockSpec((1, block, block), lambda i, s: (i, 0, 0))
    full = jax.ShapeDtypeStruct((length, channels), F32)
    return pl.pallas_call(
        local_body,
        grid_spec=pltpu.PrefetchScalarGridSpec(
            num_scalar_prefetch=1,
            grid=(blocks,),
            in_specs=[
                rows(length),
                rows(HALO),
                rows(hist.shape[0]),
                rows(conv_w.shape[0]),
                gate,
                gate,
                rows(1),
                rows(1),
                rows(1),
            ],
            out_specs=[rows(length)] * 7 + [rows(16), rows(8), rows(HALO)],
            scratch_shapes=[pltpu.VMEM((length + 8, block), F32)]
            + [pltpu.VMEM((block // LANES, length, LANES), F32)] * 5,
        ),
        out_shape=[jax.ShapeDtypeStruct((length, channels), BF16)]
        + [full] * 6
        + [
            jax.ShapeDtypeStruct((16, channels), F32),
            jax.ShapeDtypeStruct((8, channels), F32),
            jax.ShapeDtypeStruct((HALO, channels), F32),
        ],
        compiler_params=params(),
        cost_estimate=cost(4 * length * channels * block, 28 * length * channels),
        name="local",
    )(where, projected, tail, hist, conv_w, ga, gi, ab, ib, rate)


def unpack(got, pieces):
    got[0, :, :] = pieces[0][...]
    got[1, :, :] = pieces[1][...]
    for p in range(1, len(pieces) - 1):
        got[2 * p, :, :] = pieces[p + 1][0:8, :]
        got[2 * p + 1, :, :] = pieces[p + 1][8:16, :]


def states_body(pairs, where, *refs):
    pieces, refs = refs[: pairs + 1], refs[pairs + 1 :]
    init_ref, ends_ref, sl_ref, dc_ref, branch_ref, states_ref, gated_ref, in_ref, got = refs
    length, width = sl_ref.shape
    me, count, per = where[2], 2 * pairs, length // CHUNKS
    unpack(got, pieces)
    enter = init_ref[...]
    for c in range(count - 1):
        item = got.at[jnp.bitwise_xor(me, c)]
        enter = jnp.where(c < me, item[0:1, :] * enter + item[1:2, :], enter)
    in_ref[...] = jnp.broadcast_to(enter, (8, width))
    for j in range(CHUNKS):
        rows = slice(j * per, (j + 1) * per)
        states = sl_ref[rows, :] + dc_ref[rows, :] * enter
        states_ref[rows, :] = states
        gated_ref[rows, :] = (states * branch_ref[rows, :].astype(F32)).astype(BF16)
        enter = ends_ref[8 + j : 9 + j, :] * enter + ends_ref[j : j + 1, :]


def make_states(where, pieces, init, ends, sl, dc, branch):
    length, channels = sl.shape
    block = min(256, channels)
    pairs = len(pieces) - 1

    def rows(n):
        return pl.BlockSpec((n, block), lambda i, s: (0, i))

    return pl.pallas_call(
        functools.partial(states_body, pairs),
        grid_spec=pltpu.PrefetchScalarGridSpec(
            num_scalar_prefetch=1,
            grid=(channels // block,),
            in_specs=[rows(piece.shape[0]) for piece in pieces]
            + [rows(1), rows(16), rows(length), rows(length), rows(length)],
            out_specs=[rows(length), rows(length), rows(8)],
            scratch_shapes=[pltpu.VMEM((2 * pairs, 8, block), F32)],
        ),
        out_shape=[
            jax.ShapeDtypeStruct((length, channels), F32),
            jax.ShapeDtypeStruct((length, channels), BF16),
            jax.ShapeDtypeStruct((8, channels), F32),
        ],
        compiler_params=params(),
        cost_estimate=cost(4 * length * channels, 16 * length * channels),
        name="states",
    )(where, *pieces, init, ends, sl, dc, branch)


def gate_grads(adjoint, previous, conv_wide, recur, inp, rate):
    decay, remain = decays(recur, rate)
    scaler = jnp.sqrt(remain)
    scaler_grad = adjoint * inp * conv_wide
    log_grad = adjoint * previous * decay - 2.0 * decay * decay * scaler_grad * lax.rsqrt(
        jnp.maximum(4.0 * remain, 1e-06)
    )
    recur_pre = (log_grad * (-8.0 * rate) * recur * (1.0 - recur)).astype(BF16)
    input_pre = (scaler_grad * scaler * (1.0 - inp)).astype(BF16)
    return log_grad, recur_pre, input_pre, adjoint * scaler * inp


def final_body(
    pairs,
    where,
    *refs,
):
    forward, refs = refs[: pairs + 1], refs[pairs + 1 :]
    backward, refs = refs[: pairs + 1], refs[pairs + 1 :]
    (
        halo_ref,
        in_ref,
        ends_ref,
        back_ends_ref,
        proj_ref,
        tail_ref,
        hist_ref,
        conv_w_ref,
        ga_ref,
        gi_ref,
        rate_ref,
        grad_ref,
        conv_ref,
        recur_ref,
        input_ref,
        states_ref,
        al_ref,
        qq_ref,
        branch_grad_ref,
        proj_grad_ref,
        sums_a_ref,
        sums_i_ref,
        ext,
        cgr,
        adj,
        prev,
        got,
        got_back,
    ) = refs
    length, width = proj_ref.shape
    taps = conv_w_ref.shape[0]
    n = taps - 1
    me = where[2]
    count = 2 * pairs
    unpack(got, forward)
    unpack(got_back, backward)
    carry_in = jnp.zeros((1, width), F32)
    next_in = jnp.zeros((1, width), F32)
    for c in range(count - 1, 0, -1):
        at = jnp.bitwise_xor(me, c)
        longer = got.at[at][0:1, :] * carry_in + got_back.at[at][0:1, :]
        next_in = jnp.where(c == me + 1, carry_in, next_in)
        carry_in = jnp.where(c > me, longer, carry_in)
    per = length // CHUNKS
    states = states_ref[...]
    prev[7:8, :] = in_ref[0:1, :]
    prev[8 : 8 + length, :] = states
    back = carry_in
    for j in range(CHUNKS - 1, -1, -1):
        rows = slice(j * per, (j + 1) * per)
        adj[rows, :] = al_ref[rows, :] + qq_ref[rows, :] * back
        back = ends_ref[8 + j : 9 + j, :] * back + back_ends_ref[j : j + 1, :]
    branch_grad_ref[...] = (grad_ref[...] * states).astype(BF16)
    rate = rate_ref[...]
    conv_out = conv_ref[...]
    recur = recur_ref[...]
    log_grad, recur_pre, input_pre, direct = gate_grads(
        adj[...], prev[7 : 7 + length, :], conv_out.astype(F32), recur, input_ref[...], rate
    )
    conv_grad = direct + dot_nt(recur_pre, ga_ref[0]) + dot_nt(input_pre, gi_ref[0])
    cgr[0:length, :] = conv_grad
    conv_n, recur_n, inp_n = (halo_ref[k * n : (k + 1) * n, :] for k in range(3))
    after_me = got_back.at[jnp.bitwise_xor(me, lax.rem(me + 1, count))]
    adj_n = after_me[1 : 1 + n, :] + halo_ref[3 * n : 4 * n, :] * next_in
    decay_n, remain_n = decays(recur_n, rate)
    drive_n = jnp.sqrt(remain_n) * inp_n * conv_n
    run = states[length - 1 : length]
    before = [run]
    for t in range(n - 1):
        run = decay_n[t : t + 1] * run + drive_n[t : t + 1]
        before.append(run)
    _, recur_e, input_e, direct_e = gate_grads(
        adj_n, jnp.concatenate(before, 0), conv_n, recur_n, inp_n, rate
    )
    empty = jnp.zeros((8 - n, width), F32)

    def padded(value):
        return jnp.concatenate([value.astype(F32), empty], 0)

    ext_grad = (
        padded(direct_e)
        + dot_nt(padded(recur_e).astype(BF16), ga_ref[0])
        + dot_nt(padded(input_e).astype(BF16), gi_ref[0])
    )
    cgr[length : length + 8, :] = jnp.where(me == count - 1, 0.0, ext_grad)
    fill_ext(ext, proj_ref, tail_ref, hist_ref, me == 0)
    kernel = conv_w_ref[...].astype(F32)
    proj_sum = kernel[0:1] * conv_grad
    tap_sums = [jnp.sum(conv_grad * ext[8 : 8 + length, :], 0, keepdims=True)]
    for j in range(1, taps):
        proj_sum = proj_sum + kernel[j : j + 1] * cgr[j : j + length, :]
        tap_sums.append(jnp.sum(conv_grad * ext[8 - j : 8 - j + length, :], 0, keepdims=True))
    proj_grad_ref[...] = proj_sum.astype(BF16)
    sums_a_ref[0, 0:width, :] = dot_tn(conv_out, recur_pre).astype(BF16)
    sums_i_ref[0, 0:width, :] = dot_tn(conv_out, input_pre).astype(BF16)
    other_sums = [
        jnp.sum(log_grad * (-8.0 * recur), 0, keepdims=True),
        jnp.sum(recur_pre.astype(F32), 0, keepdims=True),
        jnp.sum(input_pre.astype(F32), 0, keepdims=True),
    ]
    pad_a = jnp.zeros((SUMS - taps, width), F32)
    pad_i = jnp.zeros((SUMS - 3, width), F32)
    sums_a_ref[0, width : width + SUMS, :] = jnp.concatenate(tap_sums + [pad_a], 0).astype(BF16)
    sums_i_ref[0, width : width + SUMS, :] = jnp.concatenate(other_sums + [pad_i], 0).astype(BF16)


def final(
    where, forward, backward, halo, entered, ends, back_ends, projected, tail, hist, conv_w,
    ga, gi, rate, grad, kept,
):
    length, channels = projected.shape
    blocks, block = ga.shape[0], ga.shape[1]
    pairs = len(forward) - 1

    def rows(n):
        return pl.BlockSpec((n, block), lambda i, s: (0, i))

    gate = pl.BlockSpec((1, block, block), lambda i, s: (i, 0, 0))
    sums = pl.BlockSpec((1, block + SUMS, block), lambda i, s: (i, 0, 0))
    half = jax.ShapeDtypeStruct((length, channels), BF16)
    summed = jax.ShapeDtypeStruct((blocks, block + SUMS, block), BF16)
    tall = pltpu.VMEM((length + 8, block), F32)
    few = pltpu.VMEM((2 * pairs, 8, block), F32)
    return pl.pallas_call(
        functools.partial(final_body, pairs),
        grid_spec=pltpu.PrefetchScalarGridSpec(
            num_scalar_prefetch=1,
            grid=(blocks,),
            in_specs=[rows(piece.shape[0]) for piece in (*forward, *backward)]
            + [
                rows(HALO),
                rows(8),
                rows(16),
                rows(CHUNKS),
                rows(length),
                rows(HALO),
                rows(hist.shape[0]),
                rows(conv_w.shape[0]),
                gate,
                gate,
                rows(1),
                rows(length),
            ]
            + [rows(length)] * 6,
            out_specs=[rows(length)] * 2 + [sums] * 2,
            scratch_shapes=[tall, tall, pltpu.VMEM((length, block), F32), tall, few, few],
        ),
        out_shape=[half, half, summed, summed],
        compiler_params=params(),
        cost_estimate=cost(8 * length * channels * block, 36 * length * channels),
        name="final",
    )(
        where, *forward, *backward, halo, entered, ends, back_ends, projected, tail, hist,
        conv_w, ga, gi, rate, grad, *kept,
    )


def back_body(count, where, pg_ref, w_ref, *refs):
    outs, (acc, held, w_sem) = refs[:count], refs[count:]
    rows = outs[0].shape[0]
    loads = weights(w_ref, held, w_sem, 0)

    @pl.when(pl.program_id(0) == 0)
    def _():
        for copy in loads:
            copy.start()

    ready(loads)
    acc[...] = dot_nt(pg_ref[...], held[pl.program_id(0)])
    for d, out in enumerate(outs):
        place = lax.rem(where[0] + d, count) * rows
        out[...] = acc[pl.ds(pl.multiple_of(place, rows), rows), :].astype(BF16)


def token_parts(where, proj_grad, w_in, count):
    length, channels = proj_grad.shape
    depth = w_in.shape[0]
    tile = min(1024, depth)
    rows = length // count
    return pl.pallas_call(
        functools.partial(back_body, count),
        grid_spec=pltpu.PrefetchScalarGridSpec(
            num_scalar_prefetch=1,
            grid=(depth // tile,),
            in_specs=[
                pl.BlockSpec((length, channels), lambda n, s: (0, 0)),
                HBM,
            ],
            out_specs=[pl.BlockSpec((rows, tile), lambda n, s: (0, n))] * count,
            scratch_shapes=[
                pltpu.VMEM((length, tile), F32),
                pltpu.VMEM((depth // tile, tile, channels), BF16),
                pltpu.SemaphoreType.DMA((depth // tile,)),
            ],
        ),
        out_shape=[jax.ShapeDtypeStruct((rows, depth), BF16)] * count,
        compiler_params=params(),
        cost_estimate=cost(2 * length * depth * channels, 2 * depth * (channels + length)),
        name="back",
    )(where, proj_grad, w_in)


def spread(parts, chosen):
    return {k: swap(parts[k], "ctx", 2 * k) for k in chosen}


def gather_z(value, axis):
    size = lax.axis_size(axis)
    if size != 4:
        return [value] + [shift(value, axis, d) for d in range(1, size)]
    far = shift(value, axis, 2)
    plus = step(value, axis, 1)
    minus = step(value, axis, -1)
    relayed = lax.ppermute(far, axis, [(2, 3), (1, 0)])
    return [value, far, plus, minus, relayed]


def exchange(sent, chips):
    paired = swap(sent, "ctx", 1)
    both = jnp.concatenate([sent, paired], 0)
    return [sent, paired] + [swap(both, "ctx", 2 * k) for k in range(1, chips)]


def shards(
    tokens,
    branch,
    out_grad,
    w_in,
    conv_w,
    gate_a_w,
    gate_a_b,
    gate_i_w,
    gate_i_b,
    decay_param,
    w_out,
    state_init,
    conv_history,
):
    groups, runs = lax.axis_size("mp"), lax.axis_size("ctx")
    chips = runs // 2
    here, run = lax.axis_index("mp"), lax.axis_index("ctx")
    core = lax.rem(run, 2)
    where = jnp.stack([here, run // 2, run, core]).astype(jnp.int32)
    channels = w_in.shape[1]
    blocks, block = gate_a_w.shape[0], gate_a_w.shape[1]
    taps = conv_w.shape[0]
    rate = jax.nn.softplus(-decay_param).reshape(1, channels)
    slope = -jax.nn.sigmoid(-decay_param)
    a_b, i_b = gate_a_b.reshape(1, channels), gate_i_b.reshape(1, channels)
    init = state_init.reshape(1, channels)

    near, far = list(range(1, chips - 1)), list(range(chips - 1, chips))
    chip = run // 2
    parts = gather_z(tokens, "mp")
    wide = out_grad.shape[1] // chips
    grad_cols = [
        lax.dynamic_slice_in_dim(out_grad, jnp.bitwise_xor(chip, k) * wide, wide, 1)
        for k in range(chips)
    ]
    grad_got = spread(grad_cols, near + far)
    grad_own = jnp.concatenate([grad_cols[0]] + [grad_got[k] for k in range(1, chips)], 0)
    projected, tail, *token_cols = project(where, parts, w_in, groups, chips)
    grad_parts = gather_z(out_grad, "mp")
    tail = step(tail, "ctx", 1)
    token_got = spread(token_cols, near + far)
    *kept, qq, ends, sent, halo = local(
        where, projected, tail, conv_history, conv_w, gate_a_w, gate_i_w, a_b, i_b, rate
    )
    conv_out, recur, inp, dec, sl, dc = kept
    forward = exchange(sent, chips)
    halo = step(halo, "ctx", -1)
    states, gated, entered = make_states(where, forward, init, ends, sl, dc, branch)
    gated_got = spread([gated] * chips, near + far)
    grad, al, back_ends, sent = grads(
        where, grad_parts, w_out, dec, qq[:8], ends, branch, groups
    )
    grad_cols = gather_z(grad_own, "mp")
    backward = exchange(sent, chips)
    branch_grad, proj_grad, sums_a, sums_i = final(
        where, forward, backward, halo, entered, ends, back_ends, projected, tail, conv_history,
        conv_w, gate_a_w, gate_i_w, rate, grad, (conv_out, recur, inp, states, al, qq),
    )
    parts_out = token_parts(where, proj_grad, w_in, groups)
    received = [parts_out[0]] + [shift(parts_out[d], "mp", d) for d in far_first(groups)]
    tokens_grad = sum(part.astype(F32) for part in received).astype(BF16)
    proj_got = spread([proj_grad] * chips, near + far)

    def pieces(own, got):
        return [own] + [got[k] for k in range(1, chips)]

    other_out, mine_out = weigh(where, pieces(gated, gated_got), grad_cols, "out", groups)
    w_out_grad = mine_out + swap(other_out, "ctx", 1).astype(F32)
    other_in, mine_in = weigh(
        where, pieces(token_cols[0], token_got), pieces(proj_grad, proj_got), "in", groups
    )
    w_in_grad = mine_in + swap(other_in, "ctx", 1).astype(F32)

    sums_mine = jnp.where(core == 0, sums_a, sums_i).astype(F32)
    sums_other = jnp.where(core == 0, sums_i, sums_a)
    chip_sum = (sums_mine + swap(sums_other, "ctx", 1).astype(F32)).astype(BF16)
    rows = blocks * (block + SUMS) // chips
    pieces = chip_sum.reshape(chips, rows, block)
    total = lax.dynamic_index_in_dim(pieces, chip, 0, False).astype(F32)
    for k in range(1, chips):
        piece = lax.dynamic_index_in_dim(pieces, jnp.bitwise_xor(chip, k), 0, False)
        total = total + swap(piece, "ctx", 2 * k).astype(F32)
    total = total.astype(BF16)
    result = jnp.zeros((chips, rows, block), BF16)
    result = lax.dynamic_update_index_in_dim(result, total, chip, 0)
    for k in range(1, chips):
        result = lax.dynamic_update_index_in_dim(
            result, swap(total, "ctx", 2 * k), jnp.bitwise_xor(chip, k), 0
        )
    result = result.reshape(blocks, block + SUMS, block)
    partner = swap(result, "ctx", 1)
    all_a = jnp.where(core == 0, result, partner).astype(F32)
    all_i = jnp.where(core == 0, partner, result).astype(F32)
    conv_w_grad = all_a[:, block : block + taps].transpose(1, 0, 2).reshape(taps, channels)
    rate_total = all_i[:, block].reshape(channels)
    return (
        tokens_grad,
        branch_grad,
        w_in_grad,
        w_out_grad,
        conv_w_grad,
        all_a[:, :block],
        all_i[:, block + 1].reshape(channels),
        all_i[:, :block],
        all_i[:, block + 2].reshape(channels),
        rate_total * slope,
    )


def solution(mesh):
    placed = (
        P(("ctx", "mp"), None),
        P("ctx", "mp"),
        P(("ctx", "mp"), None),
        P(None, "mp"),
        P(None, "mp"),
        P("mp", None, None),
        P("mp"),
        P("mp", None, None),
        P("mp"),
        P("mp"),
        P("mp", None),
        P("mp"),
        P(None, "mp"),
    )
    return jax.shard_map(
        shards,
        mesh=mesh,
        in_specs=placed,
        out_specs=(
            P(("ctx", "mp"), None),
            P("ctx", "mp"),
            P("ctx", "mp"),
            P("mp", "ctx"),
            P(None, "mp"),
            P("mp", None, None),
            P("mp"),
            P("mp", None, None),
            P("mp"),
            P("mp"),
        ),
        check_vma=False,
    )
```
